32 devices in a mesh: row: 2 (over x), col: 16 (over z, y, core).
Axes of the slice: x: 2, y: 2, z: 4, core: 2. Of those that a mesh axis runs over, the one named last changes fastest.
Arguments:
- chol_window: bfloat16 [512, 8, 1024], P('row', None, 'col'), may hold values from -6 to 6
- pair_vectors: bfloat16 [512, 512, 1024], P('row', 'col'), may hold values from -0.1875 to 0.1875
- amplitudes: bfloat16 [512, 512, 256], P('row', 'col'), may hold values from -0.015625 to 0.015625
Outputs:
- ladder: float32 [8, 256, 512], P(None, 'col', 'row')
The draws below stay inside these ranges and needn't reach their ends.
All inputs are finite; a program needn't handle non-finite values.
Results may differ from the reference program's by a relative error of at most 0.0029.
Values may be sent and summed in bfloat16 or wider, within the bound.
A program may use at most 320 MiB of HBM per device.

```python
import jax
import jax.numpy as jnp
from jax import lax

V = 512
NQ = 1024
NA = 8
NP = 256


def strengthened(result, rng, source, target, shards_of, factor):
    def block_of(axis_at):
        return (jnp.arange(result.shape[axis_at]) // (result.shape[axis_at] // shards_of)).reshape((-1,) + (1,) * (result.ndim - 1 - axis_at))

    first = jax.random.permutation(rng, shards_of)[block_of(target)]
    second = (block_of(target) + shards_of // 2) % shards_of
    return jnp.where((block_of(source) == first) | (block_of(source) == second), factor * result, result)


def shard_levels(rng, dims, pieces, low, largest):
    def one(position, blocks):
        draws = jax.random.uniform(jax.random.fold_in(jax.random.fold_in(rng, 6), position), (blocks,), jnp.float32, low / len(pieces), largest / len(pieces))
        return jnp.repeat(jnp.exp(draws), dims[position] // blocks).reshape((-1,) + (1,) * (len(dims) - position - 1))

    level = one(*pieces[0])
    for cut in pieces[1:]:
        level = level * one(*cut)
    return level


def centred(key, shape, spread, bound, pieces=(), dtype=jnp.bfloat16):
    level = shard_levels(key, shape, pieces, -0.22, 0.18) if pieces else 1.0
    array = jax.random.normal(key, shape, jnp.float32) * spread * level
    return jnp.minimum(jnp.maximum(array, -bound), bound).astype(dtype)


def gaussian_with(key, dims, deviation, limit, shards, heavy, dtype=jnp.bfloat16):
    drawn = deviation * jax.random.normal(key, dims, jnp.float32)
    if shards:
        drawn = drawn * shard_levels(key, dims, shards, -0.22, 0.18)
    return jnp.clip(strengthened(drawn, jax.random.fold_in(key, 3), *heavy), -limit, limit).astype(dtype)


def setup_inputs(seed: int = 0) -> dict:
    key_of = jax.random.split(jax.random.key(seed), 4)
    chol_window = centred(key_of[0], (V, NA, NQ), 1.0, 6.0, ((0, 2), (2, 16)))
    pair_vectors = centred(key_of[1], (V, V, NQ), NQ ** -0.5, 0.1875, ((0, 2), (1, 16)))
    amplitudes = gaussian_with(key_of[2], (V, V, NP), (V * V) ** -0.5, 0.015625, ((0, 2), (1, 16)), (1, 2, 16, 2.0))
    return dict(chol_window=chol_window, pair_vectors=pair_vectors, amplitudes=amplitudes)


def reference(chol_window, pair_vectors, amplitudes):
    block_rows = 16
    flat_window = chol_window.reshape(V * NA, NQ)
    stacked = pair_vectors.reshape(V // block_rows, block_rows * V, NQ)
    amps_wide = amplitudes.astype(jnp.float32)

    def one_block(vectors):
        integrals = lax.dot_general(flat_window, vectors, (((1,), (1,)), ((), ())), preferred_element_type=jnp.float32)
        integrals = integrals.astype(jnp.bfloat16).astype(jnp.float32).reshape(V, NA, block_rows, V)
        return jnp.einsum("cabd,cdn->anb", integrals, amps_wide, precision=lax.Precision.HIGHEST)

    pieces_out = lax.map(one_block, stacked)
    return pieces_out.transpose(1, 2, 0, 3).reshape(NA, NP, V)
```

```python
import functools

import jax
import jax.numpy as jnp
from jax import lax
from jax.experimental import pallas as pl
from jax.experimental.pallas import tpu as pltpu
from jax.sharding import PartitionSpec as P

A_GROUPS = 4
D_BLOCK = 4


def ladder_kernel(c, last, first, p_ref, w_ref, t_ref, *rest):
    if first:
        out_ref, it, acc = rest
    else:
        prev_ref, out_ref, it, acc = rest
    step = pl.program_id(0)
    d_block, b, q = p_ref.shape
    groups = w_ref.shape[1] // c
    n = t_ref.shape[2]

    @pl.when(step == 0)
    def _():
        acc[...] = jnp.zeros_like(acc) if first else prev_ref[...]

    rows = p_ref[...].reshape(d_block * b, q)
    for a in range(groups):
        term = jnp.dot(rows, w_ref[:, a * c:(a + 1) * c], preferred_element_type=jnp.float32)
        term = term.astype(jnp.bfloat16)
        for d in range(d_block):
            it[a * b:(a + 1) * b, d * c:(d + 1) * c] = term[d * b:(d + 1) * b]
    acc[...] += jnp.dot(it[...], t_ref[...].reshape(d_block * c, n), preferred_element_type=jnp.float32)

    @pl.when(step == pl.num_programs(0) - 1)
    def _():
        out_ref[...] = acc[...].T if last else acc[...]


def ladder_call(p_t, w, t, prev, last):
    d, b, q = p_t.shape
    c, n = t.shape[1], t.shape[2]
    width = w.shape[1]
    rows = width // c * b
    d_block = D_BLOCK if d % D_BLOCK == 0 else 1
    out = (n, rows) if last else (rows, n)
    whole = lambda shape: pl.BlockSpec(shape, lambda i: (0,) * len(shape))
    in_specs = [
        pl.BlockSpec((d_block, b, q), lambda i: (i, 0, 0)),
        whole((q, width)),
        pl.BlockSpec((d_block, c, n), lambda i: (i, 0, 0)),
    ]
    args = [p_t, w, t]
    if prev is not None:
        in_specs.append(whole((rows, n)))
        args.append(prev)
    flops = 2 * d * b * width * (q + n)
    return pl.pallas_call(
        functools.partial(ladder_kernel, c, last, prev is None),
        out_shape=jax.ShapeDtypeStruct(out, jnp.float32),
        grid=(d // d_block,),
        in_specs=in_specs,
        out_specs=whole(out),
        scratch_shapes=[
            pltpu.VMEM((rows, d_block * c), jnp.bfloat16),
            pltpu.VMEM((rows, n), jnp.float32),
        ],
        cost_estimate=pl.CostEstimate(flops=flops, bytes_accessed=2 * (p_t.size + w.size + t.size), transcendentals=0),
        compiler_params=pltpu.CompilerParams(vmem_limit_bytes=56 * 2**20),
    )(*args)


def local(row_count, chol_window, pair_vectors, amplitudes):
    c, width_a, q_own = chol_window.shape
    b = pair_vectors.shape[0]
    groups = A_GROUPS if width_a % A_GROUPS == 0 else 1
    per = width_a // groups

    w_own = chol_window.transpose(2, 1, 0)
    t_own = amplitudes.transpose(1, 0, 2)
    if row_count == 1:
        blocks = [(w_own, t_own)]
    elif c % 128 == 0:
        blocks = [(w_own, t_own)]
        for shift in range(1, row_count):
            pairs = [(i, (i + shift) % row_count) for i in range(row_count)]
            blocks.append((lax.ppermute(w_own, "row", pairs), lax.ppermute(t_own, "row", pairs)))
    else:
        blocks = [(
            lax.all_gather(w_own, "row", axis=2, tiled=True),
            lax.all_gather(t_own, "row", axis=1, tiled=True),
        )]
    p_t = pair_vectors.transpose(1, 0, 2)

    sums = [None] * groups
    for index, (w, t) in enumerate(blocks):
        for g in range(groups):
            piece = w[:, g * per:(g + 1) * per].reshape(q_own, -1)
            piece = lax.all_gather(piece, "col", axis=0, tiled=True)
            sums[g] = ladder_call(p_t, piece, t, sums[g], index == len(blocks) - 1)
    parts = [lax.psum_scatter(s, "col", scatter_dimension=0, tiled=True) for s in sums]
    parts = [s.reshape(s.shape[0], per, b).transpose(1, 0, 2) for s in parts]
    return jnp.concatenate(parts, axis=0)


def solution(mesh):
    return jax.shard_map(
        functools.partial(local, mesh.shape["row"]),
        mesh=mesh,
        in_specs=(P("row", None, "col"), P("row", "col", None), P("row", "col", None)),
        out_specs=P(None, "col", "row"),
        check_vma=False,
    )
```

```python
import functools

import jax
import jax.numpy as jnp
from jax import lax
from jax.experimental import pallas as pl
from jax.experimental.pallas import tpu as pltpu
from jax.sharding import PartitionSpec as P

MESH = pl.DeviceIdType.MESH
D_BLOCK = 4


def ladder_kernel(c, last, first, p_ref, w_ref, t_ref, *rest):
    if first:
        out_ref, it, acc = rest
    else:
        prev_ref, out_ref, it, acc = rest
    step = pl.program_id(0)
    d_block, b, q = p_ref.shape
    groups = w_ref.shape[1] // c
    n = t_ref.shape[2]

    @pl.when(step == 0)
    def _():
        acc[...] = jnp.zeros_like(acc) if first else prev_ref[...]

    rows = p_ref[...].reshape(d_block * b, q)
    for a in range(groups):
        term = jnp.dot(rows, w_ref[:, a * c:(a + 1) * c], preferred_element_type=jnp.float32)
        term = term.astype(jnp.bfloat16)
        for d in range(d_block):
            it[a * b:(a + 1) * b, d * c:(d + 1) * c] = term[d * b:(d + 1) * b]
    acc[...] += jnp.dot(it[...], t_ref[...].reshape(d_block * c, n), preferred_element_type=jnp.float32)

    @pl.when(step == pl.num_programs(0) - 1)
    def _():
        out_ref[...] = acc[...].T.astype(out_ref.dtype) if last else acc[...]


def ladder_call(p_t, w, t, prev, last):
    d, b, q = p_t.shape
    c, n = t.shape[1], t.shape[2]
    width = w.shape[1]
    rows = width // c * b
    d_block = D_BLOCK if d % D_BLOCK == 0 else 1
    out = (n, rows) if last else (rows, n)
    whole = lambda shape: pl.BlockSpec(shape, lambda i: (0,) * len(shape))
    in_specs = [
        pl.BlockSpec((d_block, b, q), lambda i: (i, 0, 0)),
        whole((q, width)),
        pl.BlockSpec((d_block, c, n), lambda i: (i, 0, 0)),
    ]
    args = [p_t, w, t]
    if prev is not None:
        in_specs.append(whole((rows, n)))
        args.append(prev)
    flops = 2 * d * b * width * (q + n)
    return pl.pallas_call(
        functools.partial(ladder_kernel, c, last, prev is None),
        out_shape=jax.ShapeDtypeStruct(out, jnp.bfloat16 if last else jnp.float32),
        grid=(d // d_block,),
        in_specs=in_specs,
        out_specs=whole(out),
        scratch_shapes=[
            pltpu.VMEM((rows, d_block * c), jnp.bfloat16),
            pltpu.VMEM((rows, n), jnp.float32),
        ],
        cost_estimate=pl.CostEstimate(flops=flops, bytes_accessed=2 * (p_t.size + w.size + t.size), transcendentals=0),
        compiler_params=pltpu.CompilerParams(vmem_limit_bytes=60 * 2**20),
    )(*args)


def scatter_kernel(cols, x_ref, out_ref, held, send_sem, recv_sem):
    me = lax.axis_index("col")
    barrier = pltpu.get_barrier_semaphore()
    for s in range(1, cols):
        pl.semaphore_signal(barrier, inc=1, device_id={"col": lax.rem(me + s, cols)}, device_id_type=MESH)
    pl.semaphore_wait(barrier, cols - 1)
    copies = []
    for s in range(1, cols):
        to = lax.rem(me + s, cols)
        copy = pltpu.make_async_remote_copy(
            src_ref=x_ref.at[to],
            dst_ref=held.at[s - 1],
            send_sem=send_sem.at[s - 1],
            recv_sem=recv_sem.at[s - 1],
            device_id={"col": to},
            device_id_type=MESH,
        )
        copy.start()
        copies.append(copy)
    total = x_ref[me].astype(jnp.float32)
    for s, copy in enumerate(copies):
        copy.wait_recv()
        total = total + held[s].astype(jnp.float32)
    out_ref[...] = total
    for copy in copies:
        copy.wait_send()


def scatter_call(x, cols):
    n, width = x.shape
    piece = (n // cols, width)
    return pl.pallas_call(
        functools.partial(scatter_kernel, cols),
        out_shape=jax.ShapeDtypeStruct(piece, jnp.float32),
        in_specs=[pl.BlockSpec(memory_space=pltpu.VMEM)],
        out_specs=pl.BlockSpec(memory_space=pltpu.VMEM),
        scratch_shapes=[
            pltpu.VMEM((cols - 1, *piece), x.dtype),
            pltpu.SemaphoreType.DMA((cols - 1,)),
            pltpu.SemaphoreType.DMA((cols - 1,)),
        ],
        compiler_params=pltpu.CompilerParams(collective_id=0, has_side_effects=True),
    )(x.reshape(cols, *piece))


def local(row_count, col_count, chol_window, pair_vectors, amplitudes):
    c, width_a, q_own = chol_window.shape
    b = pair_vectors.shape[0]

    w_own = chol_window.transpose(2, 1, 0)
    t_own = amplitudes.transpose(1, 0, 2)
    if row_count == 1:
        blocks = [(w_own, t_own)]
    elif c % 128 == 0:
        blocks = [(w_own, t_own)]
        for shift in range(1, row_count):
            pairs = [(i, (i + shift) % row_count) for i in range(row_count)]
            blocks.append((lax.ppermute(w_own, "row", pairs), lax.ppermute(t_own, "row", pairs)))
    else:
        blocks = [(
            lax.all_gather(w_own, "row", axis=2, tiled=True),
            lax.all_gather(t_own, "row", axis=1, tiled=True),
        )]
    p_t = pair_vectors.transpose(1, 0, 2)

    total = None
    for index, (w, t) in enumerate(blocks):
        w = lax.all_gather(w.reshape(q_own, -1), "col", axis=0, tiled=True)
        total = ladder_call(p_t, w, t, total, index == len(blocks) - 1)
    out = scatter_call(total, col_count)
    return out.reshape(out.shape[0], width_a, b).transpose(1, 0, 2)


def solution(mesh):
    return jax.shard_map(
        functools.partial(local, mesh.shape["row"], mesh.shape["col"]),
        mesh=mesh,
        in_specs=(P("row", None, "col"), P("row", "col", None), P("row", "col", None)),
        out_specs=P(None, "col", "row"),
        check_vma=False,
    )
```

```python
import functools

import jax
import jax.numpy as jnp
from jax import lax
from jax.experimental import pallas as pl
from jax.experimental.pallas import tpu as pltpu
from jax.sharding import PartitionSpec as P

MESH = pl.DeviceIdType.MESH
D_BLOCK = 4


def ladder_kernel(c, last, first, p_ref, w_ref, t_ref, *rest):
    if first:
        out_ref, it, acc = rest
    else:
        prev_ref, out_ref, it, acc = rest
    step = pl.program_id(0)
    d_block, b, q = p_ref.shape
    groups = w_ref.shape[1] // c
    n = t_ref.shape[2]

    @pl.when(step == 0)
    def _():
        acc[...] = jnp.zeros_like(acc) if first else prev_ref[...]

    rows = p_ref[...].reshape(d_block * b, q)
    for a in range(groups):
        term = jnp.dot(rows, w_ref[:, a * c:(a + 1) * c], preferred_element_type=jnp.float32)
        term = term.astype(jnp.bfloat16)
        for d in range(d_block):
            it[a * b:(a + 1) * b, d * c:(d + 1) * c] = term[d * b:(d + 1) * b]
    acc[...] += jnp.dot(it[...], t_ref[...].reshape(d_block * c, n), preferred_element_type=jnp.float32)

    @pl.when(step == pl.num_programs(0) - 1)
    def _():
        out_ref[...] = acc[...].T if last else acc[...]


def ladder_call(p_t, w, t, prev, last):
    d, b, q = p_t.shape
    c, n = t.shape[1], t.shape[2]
    width = w.shape[1]
    rows = width // c * b
    d_block = D_BLOCK if d % D_BLOCK == 0 else 1
    out = (n, rows) if last else (rows, n)
    whole = lambda shape: pl.BlockSpec(shape, lambda i: (0,) * len(shape))
    in_specs = [
        pl.BlockSpec((d_block, b, q), lambda i: (i, 0, 0)),
        whole((q, width)),
        pl.BlockSpec((d_block, c, n), lambda i: (i, 0, 0)),
    ]
    args = [p_t, w, t]
    if prev is not None:
        in_specs.append(whole((rows, n)))
        args.append(prev)
    flops = 2 * d * b * width * (q + n)
    return pl.pallas_call(
        functools.partial(ladder_kernel, c, last, prev is None),
        out_shape=jax.ShapeDtypeStruct(out, jnp.float32),
        grid=(d // d_block,),
        in_specs=in_specs,
        out_specs=whole(out),
        scratch_shapes=[
            pltpu.VMEM((rows, d_block * c), jnp.bfloat16),
            pltpu.VMEM((rows, n), jnp.float32),
        ],
        cost_estimate=pl.CostEstimate(flops=flops, bytes_accessed=2 * (p_t.size + w.size + t.size), transcendentals=0),
        compiler_params=pltpu.CompilerParams(vmem_limit_bytes=60 * 2**20),
    )(*args)


def scatter_kernel(cols, pair, x_ref, out_ref, near, sums, far, near_send, near_recv, far_send, far_recv):
    me = lax.axis_index("col")
    pairs = cols // pair
    core, mine = lax.rem(me, pair), lax.div(me, pair)
    partner = mine * pair + lax.rem(core + 1, pair)

    def place(s):
        return lax.rem(mine + s, pairs) * pair

    barrier = pltpu.get_barrier_semaphore()
    others = [place(s) + core for s in range(1, pairs)] + [partner] * (pair - 1)
    for other in others:
        pl.semaphore_signal(barrier, inc=1, device_id={"col": other}, device_id_type=MESH)
    pl.semaphore_wait(barrier, len(others))

    order = [*range(1, pairs), 0]
    near_copies = {}
    if pair == 2:
        for s in order:
            near_copies[s] = pltpu.make_async_remote_copy(
                src_ref=x_ref.at[place(s) + lax.rem(core + 1, pair)],
                dst_ref=near.at[s],
                send_sem=near_send.at[s],
                recv_sem=near_recv.at[s],
                device_id={"col": partner},
                device_id_type=MESH,
            )
            near_copies[s].start()

    def pair_sum(s):
        own = x_ref[place(s) + core]
        if pair == 1:
            return own
        near_copies[s].wait_recv()
        return own + near[s]

    far_copies = []
    for s in range(1, pairs):
        sums[s - 1] = pair_sum(s).astype(sums.dtype)
        copy = pltpu.make_async_remote_copy(
            src_ref=sums.at[s - 1],
            dst_ref=far.at[s - 1],
            send_sem=far_send.at[s - 1],
            recv_sem=far_recv.at[s - 1],
            device_id={"col": place(s) + core},
            device_id_type=MESH,
        )
        copy.start()
        far_copies.append(copy)
    total = pair_sum(0)
    for s, copy in enumerate(far_copies):
        copy.wait_recv()
        total = total + far[s].astype(jnp.float32)
    out_ref[...] = total
    for copy in far_copies:
        copy.wait_send()
    for copy in near_copies.values():
        copy.wait_send()


def scatter_call(x, cols):
    n, width = x.shape
    piece = (n // cols, width)
    pair = 2 if cols % 2 == 0 else 1
    pairs = cols // pair
    far = max(pairs - 1, 1)
    return pl.pallas_call(
        functools.partial(scatter_kernel, cols, pair),
        out_shape=jax.ShapeDtypeStruct(piece, jnp.float32),
        in_specs=[pl.BlockSpec(memory_space=pltpu.VMEM)],
        out_specs=pl.BlockSpec(memory_space=pltpu.VMEM),
        scratch_shapes=[
            pltpu.VMEM((pairs, *piece), jnp.float32),
            pltpu.VMEM((far, *piece), jnp.bfloat16),
            pltpu.VMEM((far, *piece), jnp.bfloat16),
            pltpu.SemaphoreType.DMA((pairs,)),
            pltpu.SemaphoreType.DMA((pairs,)),
            pltpu.SemaphoreType.DMA((far,)),
            pltpu.SemaphoreType.DMA((far,)),
        ],
        compiler_params=pltpu.CompilerParams(collective_id=0, has_side_effects=True),
    )(x.reshape(cols, *piece))


def local(row_count, col_count, chol_window, pair_vectors, amplitudes):
    c, width_a, q_own = chol_window.shape
    b = pair_vectors.shape[0]

    w_own = chol_window.transpose(2, 1, 0)
    t_own = amplitudes.transpose(1, 0, 2)
    if row_count == 1:
        blocks = [(w_own, t_own)]
    elif c % 128 == 0:
        blocks = [(w_own, t_own)]
        for shift in range(1, row_count):
            pairs = [(i, (i + shift) % row_count) for i in range(row_count)]
            w_far, t_held = lax.optimization_barrier((lax.ppermute(w_own, "row", pairs), t_own))
            blocks.append((w_far, lax.ppermute(t_held, "row", pairs)))
    else:
        blocks = [(
            lax.all_gather(w_own, "row", axis=2, tiled=True),
            lax.all_gather(t_own, "row", axis=1, tiled=True),
        )]
    p_t = pair_vectors.transpose(1, 0, 2)

    total = None
    for index, (w, t) in enumerate(blocks):
        w = lax.all_gather(w.reshape(q_own, -1), "col", axis=0, tiled=True)
        total = ladder_call(p_t, w, t, total, index == len(blocks) - 1)
    out = scatter_call(total, col_count)
    return out.reshape(out.shape[0], width_a, b).transpose(1, 0, 2)


def solution(mesh):
    return jax.shard_map(
        functools.partial(local, mesh.shape["row"], mesh.shape["col"]),
        mesh=mesh,
        in_specs=(P("row", None, "col"), P("row", "col", None), P("row", "col", None)),
        out_specs=P(None, "col", "row"),
        check_vma=False,
    )
```

```python
import functools

import jax
import jax.numpy as jnp
from jax import lax
from jax.experimental import pallas as pl
from jax.experimental.pallas import tpu as pltpu
from jax.sharding import PartitionSpec as P

MESH = pl.DeviceIdType.MESH
D_BLOCK = 4


def ladder_kernel(c, last, first, p_ref, w_ref, t_ref, *rest):
    if first:
        out_ref, it, acc = rest
    else:
        prev_ref, out_ref, it, acc = rest
    step = pl.program_id(0)
    d_block, b, q = p_ref.shape
    groups = w_ref.shape[1] // c
    n = t_ref.shape[2]

    @pl.when(step == 0)
    def _():
        acc[...] = jnp.zeros_like(acc) if first else prev_ref[...]

    rows = p_ref[...].reshape(d_block * b, q)
    for a in range(groups):
        term = jnp.dot(rows, w_ref[:, a * c:(a + 1) * c], preferred_element_type=jnp.float32)
        term = term.astype(jnp.bfloat16)
        for d in range(d_block):
            it[a * b:(a + 1) * b, d * c:(d + 1) * c] = term[d * b:(d + 1) * b]
    acc[...] += jnp.dot(it[...], t_ref[...].reshape(d_block * c, n), preferred_element_type=jnp.float32)

    @pl.when(step == pl.num_programs(0) - 1)
    def _():
        out_ref[...] = acc[...].T if last else acc[...]


def ladder_call(p_t, w, t, prev, last):
    d, b, q = p_t.shape
    c, n = t.shape[1], t.shape[2]
    width = w.shape[1]
    rows = width // c * b
    d_block = D_BLOCK if d % D_BLOCK == 0 else 1
    out = (n, rows) if last else (rows, n)
    whole = lambda shape: pl.BlockSpec(shape, lambda i: (0,) * len(shape))
    in_specs = [
        pl.BlockSpec((d_block, b, q), lambda i: (i, 0, 0)),
        whole((q, width)),
        pl.BlockSpec((d_block, c, n), lambda i: (i, 0, 0)),
    ]
    args = [p_t, w, t]
    if prev is not None:
        in_specs.append(whole((rows, n)))
        args.append(prev)
    flops = 2 * d * b * width * (q + n)
    return pl.pallas_call(
        functools.partial(ladder_kernel, c, last, prev is None),
        out_shape=jax.ShapeDtypeStruct(out, jnp.float32),
        grid=(d // d_block,),
        in_specs=in_specs,
        out_specs=whole(out),
        scratch_shapes=[
            pltpu.VMEM((rows, d_block * c), jnp.bfloat16),
            pltpu.VMEM((rows, n), jnp.float32),
        ],
        cost_estimate=pl.CostEstimate(flops=flops, bytes_accessed=2 * (p_t.size + w.size + t.size), transcendentals=0),
        compiler_params=pltpu.CompilerParams(vmem_limit_bytes=60 * 2**20),
    )(*args)


def scatter_kernel(cols, pair, x_ref, out_ref, near, sums, far, near_send, near_recv, far_send, far_recv):
    me = lax.axis_index("col")
    pairs = cols // pair
    core, mine = lax.rem(me, pair), lax.div(me, pair)
    partner = mine * pair + lax.rem(core + 1, pair)

    def place(s):
        return lax.rem(mine + s, pairs) * pair

    barrier = pltpu.get_barrier_semaphore()
    others = [place(s) + core for s in range(1, pairs)] + [partner] * (pair - 1)
    for other in others:
        pl.semaphore_signal(barrier, inc=1, device_id={"col": other}, device_id_type=MESH)
    pl.semaphore_wait(barrier, len(others))

    order = [*range(1, pairs), 0]
    near_copies = {}
    if pair == 2:
        for s in order:
            near_copies[s] = pltpu.make_async_remote_copy(
                src_ref=x_ref.at[place(s) + lax.rem(core + 1, pair)],
                dst_ref=near.at[s],
                send_sem=near_send.at[s],
                recv_sem=near_recv.at[s],
                device_id={"col": partner},
                device_id_type=MESH,
            )
            near_copies[s].start()

    def pair_sum(s):
        own = x_ref[place(s) + core]
        if pair == 1:
            return own
        near_copies[s].wait_recv()
        return own + near[s]

    far_copies = []
    for s in range(1, pairs):
        sums[s - 1] = pair_sum(s).astype(sums.dtype)
        copy = pltpu.make_async_remote_copy(
            src_ref=sums.at[s - 1],
            dst_ref=far.at[s - 1],
            send_sem=far_send.at[s - 1],
            recv_sem=far_recv.at[s - 1],
            device_id={"col": place(s) + core},
            device_id_type=MESH,
        )
        copy.start()
        far_copies.append(copy)
    total = pair_sum(0)
    for s, copy in enumerate(far_copies):
        copy.wait_recv()
        total = total + far[s].astype(jnp.float32)
    b = out_ref.shape[2]
    for a in range(out_ref.shape[0]):
        out_ref[a] = total[:, a * b:(a + 1) * b]
    for copy in far_copies:
        copy.wait_send()
    for copy in near_copies.values():
        copy.wait_send()


def scatter_call(x, cols, width_a):
    n, width = x.shape
    piece = (n // cols, width)
    pair = 2 if cols % 2 == 0 else 1
    pairs = cols // pair
    far = max(pairs - 1, 1)
    return pl.pallas_call(
        functools.partial(scatter_kernel, cols, pair),
        out_shape=jax.ShapeDtypeStruct((width_a, n // cols, width // width_a), jnp.float32),
        in_specs=[pl.BlockSpec(memory_space=pltpu.VMEM)],
        out_specs=pl.BlockSpec(memory_space=pltpu.VMEM),
        scratch_shapes=[
            pltpu.VMEM((pairs, *piece), jnp.float32),
            pltpu.VMEM((far, *piece), jnp.bfloat16),
            pltpu.VMEM((far, *piece), jnp.bfloat16),
            pltpu.SemaphoreType.DMA((pairs,)),
            pltpu.SemaphoreType.DMA((pairs,)),
            pltpu.SemaphoreType.DMA((far,)),
            pltpu.SemaphoreType.DMA((far,)),
        ],
        compiler_params=pltpu.CompilerParams(collective_id=0, has_side_effects=True),
    )(x.reshape(cols, *piece))


def local(row_count, col_count, chol_window, pair_vectors, amplitudes):
    c, width_a, q_own = chol_window.shape

    w_own = chol_window.transpose(2, 1, 0)
    t_own = amplitudes.transpose(1, 0, 2)
    if row_count == 1:
        blocks = [(w_own, t_own)]
    elif c % 128 == 0:
        blocks = [(w_own, t_own)]
        for shift in range(1, row_count):
            pairs = [(i, (i + shift) % row_count) for i in range(row_count)]
            w_far, t_held = lax.optimization_barrier((lax.ppermute(w_own, "row", pairs), t_own))
            blocks.append((w_far, lax.ppermute(t_held, "row", pairs)))
    else:
        blocks = [(
            lax.all_gather(w_own, "row", axis=2, tiled=True),
            lax.all_gather(t_own, "row", axis=1, tiled=True),
        )]
    p_t = pair_vectors.transpose(1, 0, 2)

    total = None
    for index, (w, t) in enumerate(blocks):
        w = lax.all_gather(w.reshape(q_own, -1), "col", axis=0, tiled=True)
        total = ladder_call(p_t, w, t, total, index == len(blocks) - 1)
    return scatter_call(total, col_count, width_a)


def solution(mesh):
    return jax.shard_map(
        functools.partial(local, mesh.shape["row"], mesh.shape["col"]),
        mesh=mesh,
        in_specs=(P("row", None, "col"), P("row", "col", None), P("row", "col", None)),
        out_specs=P(None, "col", "row"),
        check_vma=False,
    )
```
